512 devices in a mesh: row: 32 (over x, y), col: 8 (over z_hi, core), vec: 2 (over z_lo).
Axes of the slice: x: 4, y: 8, z: 8 (z_hi: 4, z_lo: 2; z = z_hi * 2 + z_lo), core: 2. Of those that a mesh axis runs over, the one named last changes fastest.
Arguments:
- vectors: bfloat16 [131072, 256], P(('row', 'col'), 'vec'), parts along dimension 1, may hold values from -6 to 6
- tile_blocks: bfloat16 [32, 8, 32, 256, 256], P('row', 'col'), may hold values from -0.125 to 0.125
- block_rows: int32 [32, 8, 32], P('row', 'col'), may hold values from 0 to 15, as said below
- block_cols: int32 [32, 8, 32], P('row', 'col'), may hold values from 0 to 63, as said below
- counts: int32 [32, 8], P('row', 'col'), may hold values from 1 to 32, as said below
Outputs:
- filtered: bfloat16 [131072, 256], P(('row', 'col'), 'vec'), parts along dimension 1
The draws below stay inside these ranges and needn't reach their ends.
There are 2 independent parts, one for each index of `vec`. The reference program is written for one: setup_inputs(seed, part) draws one part's arguments, and reference() takes and returns one part's arrays. A program takes and returns all parts, laid end to end along the dimension named above; an argument that names none is the same for every part. Nothing has to cross between parts.
Inputs may be any that keep to these rules, and one draw needn't show every extreme that they name: The pairs (block_rows, block_cols // 2) of the 32 slots of one tile are all distinct. Within one tile, all slots whose block columns lie in the same group of 2 (same block_cols // 2) name the same block column. `counts`: some tile uses all 32 slots.
All inputs are finite; a program needn't handle non-finite values.
Results may differ from the reference program's by a relative error of at most 0.015.
Values may be sent and summed in bfloat16 or wider, within the bound.
A program may use at most 64 MiB of HBM per device.

```python
import jax
import jax.numpy as jnp
from jax import lax

B = 256
NB = 512
K = 128
MAXB = 32
DEGREE = 3
ORDER = 131072
RB = 16
PB = 2
N_ROW = 32
N_COL = 8


def pattern(key):
    base = jax.random.fold_in(key, 7)
    first_key, second_key, third_key, fourth_key = jax.random.split(base, 4)
    tile_keys = jax.random.split(first_key, N_ROW * N_COL)
    picks = jax.vmap(lambda k: jax.random.permutation(k, NB))(tile_keys)[:, :MAXB]
    picks = picks.reshape(N_ROW, N_COL, MAXB).astype(jnp.int32)
    slot_rows = (picks // N_ROW).astype(jnp.int32)
    piece_num = (picks % N_ROW).astype(jnp.int32)
    which = jax.random.randint(second_key, (N_ROW, N_COL, N_ROW), 0, PB).astype(jnp.int32)
    offset = jnp.take_along_axis(which, piece_num, axis=2)
    slot_cols = (piece_num * PB + offset).astype(jnp.int32)
    shifts = jax.random.randint(third_key, (N_ROW, N_COL), 0, 4).astype(jnp.int32)
    used = jnp.maximum(jnp.right_shift(jnp.full((N_ROW, N_COL), MAXB, jnp.int32), shifts), 1)
    busiest = jax.random.randint(fourth_key, (), 0, N_ROW * N_COL).astype(jnp.int32)
    flat_index = jnp.arange(N_ROW * N_COL, dtype=jnp.int32).reshape(N_ROW, N_COL)
    used = jnp.where(flat_index == busiest, MAXB, used).astype(jnp.int32)
    return (slot_rows, slot_cols, used)


def draw_block_rows(key, part):
    return pattern(key)[0]


def draw_block_cols(key, part):
    return pattern(key)[1]


def draw_counts(key, part):
    return pattern(key)[2]


def shard_levels(own_key, dims, pieces, low, high):
    level, own = 1.0, jax.random.fold_in(own_key, 6)
    for axis_at, blocks in pieces:
        steps = jnp.exp(jax.random.uniform(jax.random.fold_in(own, axis_at), (blocks,), jnp.float32, low / len(pieces), high / len(pieces)))
        level = level * jnp.repeat(steps, dims[axis_at] // blocks).reshape([-1 if axis == axis_at else 1 for axis in range(len(dims))])
    return level


def noise(stream_key, extent, width, reach, cuts=(), kind=jnp.bfloat16):
    gain = shard_levels(stream_key, extent, cuts, -0.22, 0.18) if cuts else 1.0
    entries = jax.random.normal(stream_key, extent, jnp.float32) * width * gain
    return jnp.minimum(jnp.maximum(entries, -reach), reach).astype(kind)


def setup_inputs(seed: int = 0, part: int = 0) -> dict:
    key_of = jax.random.split(jax.random.key(seed), 6)
    part_splits = jax.random.split(jax.random.fold_in(key_of[5], part), 6)
    vectors = noise(part_splits[0], (ORDER, K), 1.0, 6.0, ((0, 256),))
    tile_blocks = noise(key_of[1], (N_ROW, N_COL, MAXB, B, B), (B * max(1, N_COL * MAXB // (2 * RB))) ** -0.5, 0.125, ((0, 32), (1, 8)))
    block_rows = draw_block_rows(jax.random.fold_in(key_of[5], 71), part)
    block_cols = draw_block_cols(jax.random.fold_in(key_of[5], 71), part)
    counts = draw_counts(jax.random.fold_in(key_of[5], 71), part)
    return {"vectors": vectors, "tile_blocks": tile_blocks, "block_rows": block_rows, "block_cols": block_cols, "counts": counts}


center_value = 0.5
half_width = 2.0


def tile_term(tile_data, slot_rows, slot_cols, used, vec_all, tile_col):
    piece_num = slot_cols // PB
    offset = slot_cols % PB
    global_col = ((piece_num * N_COL + tile_col) * PB + offset).astype(jnp.int32)
    vec_blocks = jnp.take(vec_all, global_col, axis=0).astype(jnp.float32)
    products = jnp.einsum('sij,sjk->sik', tile_data.astype(jnp.float32), vec_blocks, precision=lax.Precision.HIGHEST)
    live = (jnp.arange(MAXB) < used).astype(jnp.float32)
    onehot = (slot_rows[None, :] == jnp.arange(RB)[:, None]).astype(jnp.float32) * live[None, :]
    term = jnp.einsum('ls,sik->lik', onehot, products, precision=lax.Precision.HIGHEST)
    return term.astype(jnp.bfloat16)


def apply_tiles(current, tile_blocks, block_rows, block_cols, counts):
    vec_all = current.reshape(NB, B, K)

    def one_row(tile_row):
        def one_col(tile_col):
            term = tile_term(tile_blocks[tile_row, tile_col], block_rows[tile_row, tile_col],
                             block_cols[tile_row, tile_col], counts[tile_row, tile_col], vec_all, tile_col)
            return term.astype(jnp.float32)
        terms = lax.map(one_col, jnp.arange(N_COL))
        return jnp.sum(terms, axis=0)

    summed = lax.map(one_row, jnp.arange(N_ROW))
    return summed.reshape(ORDER, K)


def reference(vectors, tile_blocks, block_rows, block_cols, counts):
    previous = vectors
    applied = apply_tiles(vectors, tile_blocks, block_rows, block_cols, counts)
    current = ((applied - center_value * previous.astype(jnp.float32)) / half_width).astype(jnp.bfloat16)
    for repeat in range(DEGREE - 1):
        applied = apply_tiles(current, tile_blocks, block_rows, block_cols, counts)
        following = (2.0 * (applied - center_value * current.astype(jnp.float32)) / half_width
                     - previous.astype(jnp.float32)).astype(jnp.bfloat16)
        previous, current = current, following
    return current
```

```python
import jax
import jax.numpy as jnp
from jax import lax
from jax.experimental import pallas as pl
from jax.experimental.pallas import tpu as pltpu
from jax.sharding import PartitionSpec as P

DEGREE = 3
CENTER = 0.5
MESH = pl.DeviceIdType.MESH

NX, NY, NZ = 4, 8, 4
SLOTS, RB, BLK, PIECE, LANES = 32, 16, 256, 512, 128

CUT = 152
PARTS = ((0, CUT), (CUT, BLK - CUT))


def _messages():
    msgs = []

    def add(rows, link, off, deps):
        msgs.append({"rows": rows, "link": link, "off": off, "deps": tuple(deps)})
        return len(msgs) - 1

    def rows_of(part, first, count):
        lo, n = PARTS[part]
        return (first, count, lo, n)

    def ring(axis, size, part, off, have):
        got = {0: tuple(have)}
        for sign in (1, -1):
            dep = tuple(have)
            for d in range(1, size // 2 + 1):
                o = list(off)
                o[axis] -= sign * (d - 1)
                last = d == size // 2
                rows = rows_of(part, 0 if sign > 0 else 1, 1) if last else rows_of(part, 0, 2)
                m = add(rows, (axis, sign), tuple(o), dep)
                dep = (m,)
                if last:
                    got[size // 2] = got.get(size // 2, ()) + (m,)
                else:
                    got[-sign * d] = (m,)
        return got

    for part, (first, second) in enumerate(((1, 0), (0, 1))):
        sizes = (NX, NY)
        got = ring(first, sizes[first], part, (0, 0), ())
        for d, have in got.items():
            off = [0, 0]
            off[first] = d
            ring(second, sizes[second], part, tuple(off), have)
    return msgs


def _order(msgs, row_us=0.0055, lat=1.7):
    n = len(msgs)

    def size(i):
        return msgs[i]["rows"][1] * msgs[i]["rows"][3]

    users = [[] for _ in range(n)]
    for i, m in enumerate(msgs):
        for d in m["deps"]:
            users[d].append(i)
    tail = [0.0] * n
    for i in reversed(range(n)):
        tail[i] = size(i) * row_us + lat + max((tail[u] for u in users[i]), default=0.0)
    free = {}
    arrive = [None] * n
    start = [None] * n
    left = set(range(n))
    while left:
        best = None
        for i in sorted(left):
            m = msgs[i]
            if any(arrive[d] is None for d in m["deps"]):
                continue
            t = max([free.get(m["link"], 0.0)] + [arrive[d] for d in m["deps"]])
            key = (t, -tail[i], i)
            if best is None or key < best:
                best = key
        t, _, i = best
        start[i] = t
        free[msgs[i]["link"]] = t + size(i) * row_us
        arrive[i] = free[msgs[i]["link"]] + lat
        left.discard(i)
    return sorted(range(n), key=lambda i: (start[i], i)), arrive


MSGS = _messages()
ORDER, ARRIVE = _order(MSGS)
N_MSG = len(MSGS)


def kernel(
    vec_ref, tiles_ref, cols_ref, links_ref, out_ref,
    g0, g1, g2, tiles, seg, xs, xr, zs, zr,
    in_sem, gs_sem, gr_sem, xs_sem, xr_sem, zs_sem, zr_sem,
):
    gathered = (g0, g1, g2)
    row = lax.axis_index("row")
    col = lax.axis_index("col")
    x, y = row // NY, row % NY
    zi, core = col // 2, col % 2

    def row_at(dx, dy):
        return ((x + dx + NX) % NX) * NY + (y + dy + NY) % NY

    links = {
        (0, 1): row_at(1, 0), (0, -1): row_at(-1, 0), (1, 1): row_at(0, 1), (1, -1): row_at(0, -1),
    }
    z_up = ((zi + 1) % NZ) * 2 + core
    z_down = ((zi + NZ - 1) % NZ) * 2 + core
    mate = zi * 2 + 1 - core

    tile_copy = pltpu.make_async_copy(tiles_ref, tiles, in_sem.at[0])
    own = pl.ds(row * 2, 2)
    vec_copy = pltpu.make_async_copy(vec_ref, g0.at[own], in_sem.at[1])
    vec_copy.start()
    tile_copy.start()

    barrier = pltpu.get_barrier_semaphore()
    for to in links.values():
        pl.semaphore_signal(barrier, inc=1, device_id={"row": to}, device_id_type=MESH)
    for to in (z_up, z_down, mate):
        pl.semaphore_signal(barrier, inc=1, device_id={"col": to}, device_id_type=MESH)
    seg[SLOTS] = jnp.zeros((BLK, LANES), jnp.float32)
    pl.semaphore_wait(barrier, 7)
    vec_copy.wait()

    def region(k, off, rows):
        first, count, lo, n = rows
        return gathered[k].at[pl.ds(row_at(*off) * 2 + first, count), pl.ds(lo, n)]

    def message(k, i, receive):
        m = MSGS[i]
        off = list(m["off"])
        if receive:
            off[m["link"][0]] -= m["link"][1]
        ref = region(k, off, m["rows"])
        return pltpu.make_async_remote_copy(
            src_ref=ref, dst_ref=ref, send_sem=gs_sem.at[k * N_MSG + i], recv_sem=gr_sem.at[k * N_MSG + i],
            device_id={"row": links[m["link"]]}, device_id_type=MESH,
        )

    def gather(k):
        done = set()
        for i in ORDER:
            for d in MSGS[i]["deps"]:
                if d not in done:
                    message(k, d, True).wait_recv()
                    done.add(d)
            message(k, i, False).start()
        for i in sorted(range(N_MSG), key=lambda i: ARRIVE[i]):
            if i not in done:
                message(k, i, True).wait_recv()

    def compute(k):
        g = gathered[k]

        def step(s, carry):
            v = g[cols_ref[0, 0, s]]
            seg[s] = jnp.dot(tiles[s], v, preferred_element_type=jnp.float32) + seg[links_ref[s]]
            return carry

        lax.fori_loop(0, SLOTS, step, 0)

    def block(l):
        return seg[links_ref[SLOTS + l]]

    def x_copy(k, t):
        return pltpu.make_async_remote_copy(
            src_ref=xs.at[k, t], dst_ref=xr.at[k, t], send_sem=xs_sem.at[k * NZ + t], recv_sem=xr_sem.at[k * NZ + t],
            device_id={"col": mate}, device_id_type=MESH,
        )

    def z_copy(k, i, to):
        return pltpu.make_async_remote_copy(
            src_ref=zs.at[k, i], dst_ref=zr.at[k, i], send_sem=zs_sem.at[k * 6 + i], recv_sem=zr_sem.at[k * 6 + i],
            device_id={"col": to}, device_id_type=MESH,
        )

    def scatter(k):
        targets = ((zi + 2) % NZ, (zi + 1) % NZ, (zi + NZ - 1) % NZ, zi)
        for t, z in enumerate(targets):
            for h in range(2):
                xs[k, t, pl.ds(h * BLK, BLK), :] = block((z * 2 + 1 - core) * 2 + h).astype(jnp.bfloat16)
            x_copy(k, t).start()

        def mine(t, h):
            return block((targets[t] * 2 + core) * 2 + h) + xr[k, t, pl.ds(h * BLK, BLK), :].astype(jnp.float32)

        def send(i, value, to):
            zs[k, i] = value.astype(jnp.bfloat16)
            z_copy(k, i, to).start()

        x_copy(k, 0).wait_recv()
        send(0, mine(0, 0), z_up)
        send(1, mine(0, 1), z_down)
        x_copy(k, 1).wait_recv()
        send(2, mine(1, 1), z_up)
        x_copy(k, 2).wait_recv()
        send(3, mine(2, 0), z_down)
        z_copy(k, 0, z_up).wait_recv()
        send(4, mine(1, 0) + zr[k, 0].astype(jnp.float32), z_up)
        z_copy(k, 1, z_down).wait_recv()
        send(5, mine(2, 1) + zr[k, 1].astype(jnp.float32), z_down)
        x_copy(k, 3).wait_recv()
        z_copy(k, 3, z_down).wait_recv()
        z_copy(k, 2, z_up).wait_recv()
        for h, i in ((0, 4), (1, 5)):
            z_copy(k, i, z_up).wait_recv()
            applied = mine(3, h) + zr[k, i].astype(jnp.float32) + zr[k, 3 - h].astype(jnp.float32)
            here = row * 2 + h
            now = gathered[k][here].astype(jnp.float32)
            value = applied - CENTER * now
            if k == 0:
                value = 0.5 * value
            else:
                value = value - gathered[k - 1][here].astype(jnp.float32)
            value = value.astype(jnp.bfloat16)
            if k == DEGREE - 1:
                out_ref[h] = value
            else:
                gathered[k + 1][here] = value

    for k in range(DEGREE):
        gather(k)
        if k == 0:
            tile_copy.wait()
        compute(k)
        scatter(k)
    for k in range(DEGREE):
        for i in range(N_MSG):
            message(k, i, False).wait_send()
        for t in range(NZ):
            x_copy(k, t).wait_send()
        for i in range(6):
            z_copy(k, i, z_up).wait_send()


def on_device(vectors, tile_blocks, block_rows, block_cols, counts):
    slot = jnp.arange(SLOTS, dtype=jnp.int32)
    rows = block_rows[0, 0]
    wanted = jnp.concatenate([rows, jnp.arange(RB, dtype=jnp.int32)])
    before = jnp.concatenate([slot, jnp.full((RB,), SLOTS, jnp.int32)])
    hit = (rows[None, :] == wanted[:, None]) & (slot[None, :] < jnp.minimum(before, counts[0, 0])[:, None])
    links = jnp.max(jnp.where(hit, slot[None, :], -1), axis=1)
    links = jnp.where(links < 0, SLOTS, links)
    any_spec = pl.BlockSpec(memory_space=pl.ANY)
    smem = pl.BlockSpec(memory_space=pltpu.SMEM)
    dma = pltpu.SemaphoreType.DMA
    return pl.pallas_call(
        kernel,
        out_shape=jax.ShapeDtypeStruct((2, BLK, LANES), jnp.bfloat16),
        in_specs=[any_spec, any_spec, smem, smem],
        out_specs=pl.BlockSpec(memory_space=pltpu.VMEM),
        scratch_shapes=[
            pltpu.VMEM((NX * NY * 2, BLK, LANES), jnp.bfloat16),
            pltpu.VMEM((NX * NY * 2, BLK, LANES), jnp.bfloat16),
            pltpu.VMEM((NX * NY * 2, BLK, LANES), jnp.bfloat16),
            pltpu.VMEM((SLOTS, BLK, BLK), jnp.bfloat16),
            pltpu.VMEM((SLOTS + 1, BLK, LANES), jnp.float32),
            pltpu.VMEM((DEGREE, NZ, PIECE, LANES), jnp.bfloat16),
            pltpu.VMEM((DEGREE, NZ, PIECE, LANES), jnp.bfloat16),
            pltpu.VMEM((DEGREE, 6, BLK, LANES), jnp.bfloat16),
            pltpu.VMEM((DEGREE, 6, BLK, LANES), jnp.bfloat16),
            dma((2,)),
            dma((DEGREE * N_MSG,)),
            dma((DEGREE * N_MSG,)),
            dma((DEGREE * NZ,)),
            dma((DEGREE * NZ,)),
            dma((DEGREE * 6,)),
            dma((DEGREE * 6,)),
        ],
        compiler_params=pltpu.CompilerParams(collective_id=0, has_side_effects=True),
        name="filter",
    )(vectors.reshape(2, BLK, LANES), tile_blocks[0, 0], block_cols, links).reshape(PIECE, LANES)


def solution(mesh):
    return jax.shard_map(
        on_device,
        mesh=mesh,
        in_specs=(
            P(("row", "col"), "vec"),
            P("row", "col", None, None, None),
            P("row", "col", None),
            P("row", "col", None),
            P("row", "col"),
        ),
        out_specs=P(("row", "col"), "vec"),
        check_vma=False,
    )
```
